128 devices in a mesh: req: 4 (over y), tile: 32 (over x, z, core).
Axes of the slice: x: 4, y: 4, z: 4, core: 2. Of those that a mesh axis runs over, the one named last changes fastest.
Arguments:
- image: bfloat16 [8, 4096, 2432], P('req', 'tile'), may hold values from -40 to 40
- text: bfloat16 [8, 154, 2432], P('req'), may hold values from -40 to 40
- pooled: float32 [8, 2432], P('req'), may hold values from -6 to 6
- timesteps: int32 [8], P('req'), may hold values from 0 to 999
- lengths: int32 [8], P('req'), may hold values from 1 to 4096, 16384 in all
- w_time: bfloat16 [256, 2432], replicated, may hold values from -0.375 to 0.375
- w_mod: bfloat16 [2432, 9728], P(None, 'tile'), may hold values from -0.125 to 0.125
- w_img: bfloat16 [2432, 6144], P(None, ('req', 'tile')), may hold values from -0.125 to 0.125
- w_txt: bfloat16 [2432, 6144], P(None, 'tile'), may hold values from -0.125 to 0.125
- q_gain: float32 [64], replicated, may hold values from 1 to 2.5
- k_gain: float32 [64], replicated, may hold values from 1 to 2.5
- text_q_gain: float32 [64], replicated, may hold values from 1 to 2.5
- text_k_gain: float32 [64], replicated, may hold values from 1 to 2.5
Outputs:
- image_attention: bfloat16 [8, 4096, 2048], P('req', 'tile')
- text_attention: bfloat16 [8, 154, 2048], P('req', None, 'tile')
The draws below stay inside these ranges and needn't reach their ends.
Inputs may be any that keep to these rules, and one draw needn't show every extreme that they name: `lengths`: the image token counts of all 8 requests sum to 16384, and the largest is exactly 4096.
All inputs are finite; a program needn't handle non-finite values. No bound on the sum of `lengths` on one device may be relied on, other than what follows from the above.
Results may differ from the reference program's by a relative error of at most 0.02.
Values may be sent and summed in bfloat16 or wider, within the bound.
A program may use at most 128 MiB of HBM per device.

```python
import math
import jax
import jax.numpy as jnp
import numpy as np
from jax import lax

D = 2432
HEADS = 32
HD = 64
FREQ = 256
TXT = 154
LMAX = 4096
REQS = 8
TOTAL = 16384


def scaled_field(key, shape):
    first, second, third = jax.random.split(key, 3)
    row_scale = jnp.exp(jax.random.uniform(second, shape[:-1] + (1,), jnp.float32, 0.0, math.log(10.0)))
    column_scale = jnp.exp(jax.random.uniform(third, (shape[-1],), jnp.float32, 0.0, math.log(10.0)))
    noise = jax.random.truncated_normal(first, -4.0, 4.0, shape, jnp.float32)
    return (noise * row_scale * column_scale * 0.1).astype(jnp.bfloat16)


def draw_image(key, part):
    return scaled_field(jax.random.fold_in(key, 11), (REQS, LMAX, D))


def draw_text(key, part):
    return scaled_field(jax.random.fold_in(key, 12), (REQS, TXT, D))


def place_ends(result, own_key, smallest, largest):
    longest = result.shape.index(max(result.shape))
    spots = []
    for shift in (0, 1):
        where = [jax.random.randint(jax.random.fold_in(own_key, axis), (), 0, length) for axis, length in enumerate(result.shape)]
        where[longest] = (where[longest] + shift) % result.shape[longest]
        spots.append(tuple(where))
    return result.at[spots[0]].set(smallest).at[spots[1]].set(largest)


def steps_of(rng, dims, cuts, smallest, high):
    def one(axis_at, blocks):
        steps = jax.random.uniform(jax.random.fold_in(jax.random.fold_in(rng, 6), axis_at), (blocks,), jnp.float32, smallest / len(cuts), high / len(cuts))
        return jnp.repeat(jnp.exp(steps), dims[axis_at] // blocks).reshape((-1,) + (1,) * (len(dims) - axis_at - 1))

    level = one(*cuts[0])
    for cut in cuts[1:]:
        level = level * one(*cut)
    return level


def profile(number_of, total, limit, skew):
    loads = [(1 << 20) // math.isqrt(grade ** skew) + 1 for grade in range(2, number_of + 1)]
    surplus, counts = total - limit - (number_of - 1), [1] * (number_of - 1)
    while surplus > 0:
        candidates = [i for i in range(number_of - 1) if counts[i] < limit]
        whole, left = sum([loads[i] for i in candidates]), surplus
        for i in candidates:
            extra = min(limit - counts[i], max(1, left * loads[i] // whole), surplus)
            counts[i] = counts[i] + extra
            surplus = surplus - extra
    return np.array([limit] + counts)


def uneven(stream_key, number_of, total, most, lean):
    if number_of == 2:
        one = jax.random.randint(stream_key, (), max(1, total - most), min(most, total - 1) + 1)
        return jnp.stack([one, total - one])
    tallies = jnp.asarray(profile(number_of, total, most, lean), jnp.int32)
    pairs = (number_of - 1) // 2
    donor, taker = tallies[1:1 + 2 * pairs:2], tallies[2:2 + 2 * pairs:2]
    slack = jnp.minimum(donor - 1, most - taker)
    passed = jax.random.randint(jax.random.fold_in(stream_key, 1), (pairs,), 0, 1 << 20) % (slack + 1)
    tallies = tallies.at[1:1 + 2 * pairs:2].set(donor - passed).at[2:2 + 2 * pairs:2].set(taker + passed)
    return tallies[jax.random.permutation(jax.random.fold_in(stream_key, 2), number_of)]


def centred(stream_key, dims, scale, reach, cuts=(), kind=jnp.bfloat16):
    values = scale * jax.random.normal(stream_key, dims, jnp.float32)
    if cuts:
        values = values * steps_of(stream_key, dims, cuts, -0.22, 0.18)
    return jnp.clip(values, -reach, reach).astype(kind)


def setup_inputs(seed: int = 0) -> dict:
    arg_keys = jax.random.split(jax.random.key(seed), 14)
    image = draw_image(jax.random.fold_in(arg_keys[13], 71), 0)
    text = draw_text(jax.random.fold_in(arg_keys[13], 71), 0)
    pooled = centred(arg_keys[2], (REQS, D), 1.0, 6.0, ((0, 4),), jnp.float32)
    timesteps = place_ends(jax.random.randint(arg_keys[3], (REQS,), 0, 1000), jax.random.fold_in(arg_keys[3], 1), 0, 999).astype(jnp.int32)
    lengths = uneven(arg_keys[4], REQS, TOTAL, LMAX, 2).astype(jnp.int32)
    w_time = centred(arg_keys[5], (FREQ, D), FREQ ** -0.5, 0.375)
    w_mod = centred(arg_keys[6], (D, 4 * D), D ** -0.5, 0.125, ((1, 32),))
    w_img = centred(arg_keys[7], (D, 3 * HEADS * HD), D ** -0.5, 0.125, ((1, 128),))
    w_txt = centred(arg_keys[8], (D, 3 * HEADS * HD), D ** -0.5, 0.125, ((1, 32),))
    q_gain = jnp.clip(jnp.exp(jax.random.uniform(arg_keys[9], (HD,), jnp.float32, math.log(1.0), math.log(2.5))), 1.0, 2.5)
    k_gain = jnp.clip(jnp.exp(jax.random.uniform(arg_keys[10], (HD,), jnp.float32, math.log(1.0), math.log(2.5))), 1.0, 2.5)
    text_q_gain = jnp.clip(jnp.exp(jax.random.uniform(arg_keys[11], (HD,), jnp.float32, math.log(1.0), math.log(2.5))), 1.0, 2.5)
    text_k_gain = jnp.clip(jnp.exp(jax.random.uniform(arg_keys[12], (HD,), jnp.float32, math.log(1.0), math.log(2.5))), 1.0, 2.5)
    return {"image": image, "text": text, "pooled": pooled, "timesteps": timesteps, "lengths": lengths, "w_time": w_time, "w_mod": w_mod, "w_img": w_img, "w_txt": w_txt, "q_gain": q_gain, "k_gain": k_gain, "text_q_gain": text_q_gain, "text_k_gain": text_k_gain}


epsilon = 1e-06

def time_features(step_index, feature_count):
    half_count = feature_count // 2
    frequency = jnp.exp(-math.log(10000.0) * jnp.arange(half_count, dtype=jnp.float32) / half_count)
    angles = step_index.astype(jnp.float32)[:, None] * frequency[None, :]
    return jnp.concatenate([jnp.cos(angles), jnp.sin(angles)], axis=-1).astype(jnp.bfloat16)

def modulate(tokens, shift, scale):
    values = tokens.astype(jnp.float32)
    center = lax.optimization_barrier(jnp.mean(values, axis=-1, keepdims=True))
    spread = lax.optimization_barrier(jnp.mean(jnp.square(values - center), axis=-1, keepdims=True))
    normed = (values - center) * lax.rsqrt(spread + epsilon)
    return (normed * (1.0 + scale.astype(jnp.float32)) + shift.astype(jnp.float32)).astype(jnp.bfloat16)

def rms_gain(vectors, gain):
    factor = lax.rsqrt(lax.optimization_barrier(jnp.mean(jnp.square(vectors), axis=-1, keepdims=True)) + epsilon)
    return (vectors * factor * gain).astype(jnp.bfloat16)

def attend(queries, keys, values, key_mask):
    scores = jnp.einsum('qe,ke->qk', queries.astype(jnp.float32), keys.astype(jnp.float32)) * HD ** (-0.5)
    weights = jnp.exp(scores) * key_mask[None, :]
    total = lax.optimization_barrier(jnp.sum(weights, axis=-1))
    summed = jnp.dot(weights.astype(jnp.bfloat16), values, preferred_element_type=jnp.float32)
    return summed / total[:, None]

def reference(image, text, pooled, timesteps, lengths, w_time, w_mod, w_img, w_txt, q_gain, k_gain, text_q_gain, text_k_gain):
    features = time_features(timesteps, FREQ)
    cond_act = jax.nn.silu(pooled + jnp.dot(features, w_time, preferred_element_type=jnp.float32)).astype(jnp.bfloat16)
    modulation = jnp.dot(cond_act, w_mod, preferred_element_type=jnp.float32).astype(jnp.bfloat16)

    def one_request(operands):
        image_one, text_one, mod_one, length_one = operands
        slot_live = (jnp.arange(LMAX, dtype=jnp.int32) < length_one).astype(jnp.float32)
        key_mask = jnp.concatenate([jnp.ones((TXT,), jnp.float32), slot_live])
        h_img = modulate(image_one, mod_one[0:D], mod_one[D:2 * D])
        h_txt = modulate(text_one, mod_one[2 * D:3 * D], mod_one[3 * D:4 * D])
        qkv_img = jnp.dot(h_img, w_img, preferred_element_type=jnp.float32).reshape(LMAX, HEADS, 3, HD)
        qkv_txt = jnp.dot(h_txt, w_txt, preferred_element_type=jnp.float32).reshape(TXT, HEADS, 3, HD)
        queries = jnp.concatenate([rms_gain(qkv_txt[:, :, 0, :], text_q_gain), rms_gain(qkv_img[:, :, 0, :], q_gain)], axis=0)
        keys = jnp.concatenate([rms_gain(qkv_txt[:, :, 1, :], text_k_gain), rms_gain(qkv_img[:, :, 1, :], k_gain)], axis=0)
        values = jnp.concatenate([qkv_txt[:, :, 2, :].astype(jnp.bfloat16), qkv_img[:, :, 2, :].astype(jnp.bfloat16)], axis=0)

        def one_head(trio):
            return attend(trio[0], trio[1], trio[2], key_mask)
        outcome = lax.map(one_head, (jnp.moveaxis(queries, 1, 0), jnp.moveaxis(keys, 1, 0), jnp.moveaxis(values, 1, 0)))
        outcome = jnp.moveaxis(outcome, 0, 1).reshape(TXT + LMAX, HEADS * HD)
        text_result = outcome[:TXT].astype(jnp.bfloat16)
        image_result = (outcome[TXT:] * slot_live[:, None]).astype(jnp.bfloat16)
        return (image_result, text_result)
    image_attention, text_attention = lax.map(one_request, (image, text, modulation, lengths))
    return (image_attention, text_attention)
```

```python
import functools
import math

import jax
import jax.numpy as jnp
from jax import lax
from jax.experimental import pallas as pl
from jax.experimental.pallas import tpu as pltpu
from jax.sharding import PartitionSpec as P

epsilon = 1e-06


def time_features(step_index, feature_count):
    half_count = feature_count // 2
    frequency = jnp.exp(-math.log(10000.0) * jnp.arange(half_count, dtype=jnp.float32) / half_count)
    angles = step_index.astype(jnp.float32)[:, None] * frequency[None, :]
    return jnp.concatenate([jnp.cos(angles), jnp.sin(angles)], axis=-1).astype(jnp.bfloat16)


def modulate(tokens, shift, scale):
    values = tokens.astype(jnp.float32)
    center = jnp.mean(values, axis=-1, keepdims=True)
    spread = jnp.mean(jnp.square(values - center), axis=-1, keepdims=True)
    normed = (values - center) * lax.rsqrt(spread + epsilon)
    return (normed * (1.0 + scale.astype(jnp.float32)) + shift.astype(jnp.float32)).astype(
        jnp.bfloat16
    )


def rms_gain(vectors, gain):
    factor = lax.rsqrt(jnp.mean(jnp.square(vectors), axis=-1, keepdims=True) + epsilon)
    return (vectors * factor * gain).astype(jnp.bfloat16)


LANES = 128
QUERY_BLOCK = 512
KEY_BLOCK = 512


def attend_kernel(lengths_ref, query_ref, key_ref, value_ref, text_key_ref, text_value_ref, out_ref, aug_ref, text_aug_ref, *, text_len, groups, width):
    step = pl.program_id(0)
    rows = query_ref.shape[0]
    seq_len = key_ref.shape[0]

    @pl.when(step == 0)
    def _():
        for group in range(groups):
            text_lane = lax.broadcasted_iota(jnp.int32, text_value_ref.shape, 1) // width == group
            text_live = lax.broadcasted_iota(jnp.int32, text_value_ref.shape, 0) < text_len
            text_value = text_value_ref[...].astype(jnp.float32)
            text_aug_ref[group] = jnp.where(
                text_live, jnp.where(text_lane, text_value, 1.0), 0.0
            ).astype(jnp.bfloat16)

            def fill(index, carry):
                start = pl.multiple_of(index * KEY_BLOCK, KEY_BLOCK)
                shape = (KEY_BLOCK, LANES)
                own = lax.broadcasted_iota(jnp.int32, shape, 1) // width == group
                live = lax.broadcasted_iota(jnp.int32, shape, 0) + start < lengths_ref[group]
                value = value_ref[pl.ds(start, KEY_BLOCK), :].astype(jnp.float32)
                aug_ref[group, pl.ds(start, KEY_BLOCK), :] = jnp.where(
                    live, jnp.where(own, value, 1.0), 0.0
                ).astype(jnp.bfloat16)
                return carry

            lax.fori_loop(0, seq_len // KEY_BLOCK, fill, 0)

    lane = lax.broadcasted_iota(jnp.int32, (rows, LANES), 1) // width
    row = lax.broadcasted_iota(jnp.int32, (rows, LANES), 0) + step * rows
    out_ref[...] = jnp.zeros_like(out_ref)
    for group in range(groups):
        length = lengths_ref[group]

        @pl.when(step * rows < length)
        def _():
            query = jnp.where(lane == group, query_ref[...].astype(jnp.float32), 0.0).astype(
                jnp.bfloat16
            )

            def part(keys, augmented):
                scores = lax.dot_general(
                    query, keys, (((1,), (1,)), ((), ())), preferred_element_type=jnp.float32
                )
                weights = jnp.exp2(scores).astype(jnp.bfloat16)
                return jnp.dot(weights, augmented, preferred_element_type=jnp.float32)

            def body(index, acc):
                start = pl.multiple_of(index * KEY_BLOCK, KEY_BLOCK)
                return acc + part(
                    key_ref[pl.ds(start, KEY_BLOCK), :],
                    aug_ref[group, pl.ds(start, KEY_BLOCK), :],
                )

            acc = part(text_key_ref[...], text_aug_ref[group])
            acc = lax.fori_loop(0, (length + KEY_BLOCK - 1) // KEY_BLOCK, body, acc)
            total = pltpu.roll(acc, LANES // 2, 1)
            result = jnp.where(row < length, acc / total, 0.0).astype(jnp.bfloat16)
            out_ref[...] = jnp.where(lane == group, result, out_ref[...])


def attend_image(lengths, by_head, text_key, text_value, text_len, groups, width):
    seq_len = by_head.shape[0]
    text_rows = text_key.shape[0]
    return pl.pallas_call(
        functools.partial(attend_kernel, text_len=text_len, groups=groups, width=width),
        grid_spec=pltpu.PrefetchScalarGridSpec(
            num_scalar_prefetch=1,
            grid=(seq_len // QUERY_BLOCK,),
            in_specs=[
                pl.BlockSpec((QUERY_BLOCK, LANES), lambda i, n: (i, 0)),
                pl.BlockSpec((seq_len, LANES), lambda i, n: (0, 1)),
                pl.BlockSpec((seq_len, LANES), lambda i, n: (0, 2)),
                pl.BlockSpec((text_rows, LANES), lambda i, n: (0, 0)),
                pl.BlockSpec((text_rows, LANES), lambda i, n: (0, 0)),
            ],
            out_specs=pl.BlockSpec((QUERY_BLOCK, LANES), lambda i, n: (i, 0)),
            scratch_shapes=[
                pltpu.VMEM((groups, seq_len, LANES), jnp.bfloat16),
                pltpu.VMEM((groups, text_rows, LANES), jnp.bfloat16),
            ],
        ),
        out_shape=jax.ShapeDtypeStruct((seq_len, LANES), jnp.bfloat16),
    )(lengths, by_head, by_head, by_head, text_key, text_value)


def local(
    image,
    text,
    pooled,
    timesteps,
    lengths,
    w_time,
    w_mod,
    w_img,
    w_txt,
    q_gain,
    k_gain,
    text_q_gain,
    text_k_gain,
):
    tile_count = lax.axis_size("tile")
    group_count, local_rows, model_width = image.shape
    seq_len = local_rows * tile_count
    text_len = text.shape[1]
    head_dim = q_gain.shape[0]
    heads_here = w_txt.shape[1] // (3 * head_dim)
    score_scale = head_dim ** (-0.5)
    same_core = [[t for t in range(tile_count) if t % 2 == c] for c in range(2)]
    all_same_core = [
        [r * tile_count + t for r in range(lax.axis_size("req")) for t in same_core[c]]
        for c in range(2)
    ]
    turned = lax.ppermute(
        w_img,
        "tile",
        [(t, t // 8 * 8 + ((t % 8) * 2 + (t % 8) // 4) % 8) for t in range(tile_count)],
    )
    w_half = lax.all_gather(
        turned, ("req", "tile"), axis=1, tiled=True, axis_index_groups=all_same_core
    )
    features = time_features(timesteps, w_time.shape[0])
    cond_act = jax.nn.silu(
        pooled + jnp.dot(features, w_time, preferred_element_type=jnp.float32)
    ).astype(jnp.bfloat16)
    mod_part = jnp.dot(cond_act, w_mod, preferred_element_type=jnp.float32).astype(jnp.bfloat16)
    modulation = lax.all_gather(mod_part, "tile", axis=1, tiled=True)
    h_img = modulate(
        image,
        modulation[:, None, 0:model_width],
        modulation[:, None, model_width : 2 * model_width],
    )
    core = lax.axis_index("tile") % 2
    h_other = lax.ppermute(h_img, "tile", [(t, t ^ 1) for t in range(tile_count)])
    h_pair = jnp.where(
        core == 0,
        jnp.concatenate([h_img, h_other], axis=1),
        jnp.concatenate([h_other, h_img], axis=1),
    )
    qkv_img = jnp.einsum("gpd,dc->gpc", h_pair, w_half, preferred_element_type=jnp.float32)
    pair_rows = 2 * local_rows
    half_heads = tile_count // 2
    qkv_img = qkv_img.reshape(group_count, pair_rows, half_heads, 3, head_dim)
    log2_scale = score_scale * math.log2(math.e)
    packed = jnp.stack(
        [
            rms_gain(qkv_img[:, :, :, 0, :], q_gain * log2_scale),
            rms_gain(qkv_img[:, :, :, 1, :], k_gain),
            qkv_img[:, :, :, 2, :].astype(jnp.bfloat16),
        ]
    )
    packed = jnp.transpose(packed, (3, 2, 0, 1, 4)).reshape(
        half_heads, pair_rows, 3 * group_count * head_dim
    )
    by_head = lax.all_to_all(
        packed, "tile", split_axis=0, concat_axis=0, tiled=True, axis_index_groups=same_core
    ).reshape(seq_len, 3 * group_count * head_dim)
    h_txt = modulate(
        text,
        modulation[:, None, 2 * model_width : 3 * model_width],
        modulation[:, None, 3 * model_width : 4 * model_width],
    )
    qkv_txt = jnp.einsum("gtd,dc->gtc", h_txt, w_txt, preferred_element_type=jnp.float32).reshape(
        group_count, text_len, heads_here, 3, head_dim
    )
    text_queries = jnp.moveaxis(rms_gain(qkv_txt[:, :, :, 0, :], text_q_gain), 2, 1)
    text_keys = jnp.moveaxis(rms_gain(qkv_txt[:, :, :, 1, :], text_k_gain), 2, 1)
    text_values = jnp.moveaxis(qkv_txt[:, :, :, 2, :].astype(jnp.bfloat16), 2, 1)
    by_part = by_head.reshape(seq_len, 3, group_count, head_dim)
    image_keys = jnp.transpose(by_part[:, 1], (1, 0, 2))[:, None]
    image_values = jnp.transpose(by_part[:, 2], (1, 0, 2))[:, None]
    slot_live = (jnp.arange(seq_len, dtype=jnp.int32)[None, :] < lengths[:, None]).astype(
        jnp.float32
    )
    keys = jnp.concatenate([text_keys, image_keys], axis=2)
    values = jnp.concatenate([text_values, image_values], axis=2)
    key_mask = jnp.concatenate([jnp.ones((group_count, text_len), jnp.float32), slot_live], axis=1)

    def attend_block(query_block):
        scores = (
            jnp.einsum("ghqe,ghke->ghqk", query_block, keys, preferred_element_type=jnp.float32)
            * score_scale
        )
        weights = jnp.exp(scores) * key_mask[:, None, None, :]
        total = jnp.sum(weights, axis=-1)
        summed = jnp.einsum(
            "ghqk,ghke->ghqe",
            weights.astype(jnp.bfloat16),
            values,
            preferred_element_type=jnp.float32,
        )
        return summed / total[..., None]

    text_result = attend_block(text_queries)
    text_rows = -(-text_len // 128) * 128

    def pack_text(vectors):
        joined = jnp.moveaxis(vectors[:, 0], 0, 1).reshape(text_len, group_count * head_dim)
        return jnp.pad(joined, ((0, text_rows - text_len), (0, 0)))

    image_result = attend_image(
        lengths, by_head, pack_text(text_keys), pack_text(text_values), text_len, group_count, head_dim
    )
    sent = image_result.reshape(tile_count, local_rows, group_count * head_dim)
    got = lax.all_to_all(sent, "tile", split_axis=0, concat_axis=0, tiled=True)
    image_attention = (
        got.reshape(tile_count, local_rows, group_count, head_dim)
        .transpose(2, 1, 0, 3)
        .reshape(group_count, local_rows, tile_count * head_dim)
    )
    text_attention = (
        jnp.moveaxis(text_result, 1, 2)
        .reshape(group_count, text_len, heads_here * head_dim)
        .astype(jnp.bfloat16)
    )
    return (image_attention, text_attention)


def solution(mesh):
    in_specs = (
        P("req", "tile", None),
        P("req", None, None),
        P("req", None),
        P("req"),
        P("req"),
        P(),
        P(None, "tile"),
        P(None, ("req", "tile")),
        P(None, "tile"),
        P(),
        P(),
        P(),
        P(),
    )
    out_specs = (P("req", "tile", None), P("req", None, "tile"))
    return jax.shard_map(local, mesh=mesh, in_specs=in_specs, out_specs=out_specs, check_vma=False)
```

```python
import functools
import math

import jax
import jax.numpy as jnp
from jax import lax
from jax.experimental import pallas as pl
from jax.experimental.pallas import tpu as pltpu
from jax.sharding import PartitionSpec as P

epsilon = 1e-06


def time_features(step_index, feature_count):
    half_count = feature_count // 2
    frequency = jnp.exp(-math.log(10000.0) * jnp.arange(half_count, dtype=jnp.float32) / half_count)
    angles = step_index.astype(jnp.float32)[:, None] * frequency[None, :]
    return jnp.concatenate([jnp.cos(angles), jnp.sin(angles)], axis=-1).astype(jnp.bfloat16)


def modulate(tokens, shift, scale):
    values = tokens.astype(jnp.float32)
    center = jnp.mean(values, axis=-1, keepdims=True)
    spread = jnp.mean(jnp.square(values - center), axis=-1, keepdims=True)
    normed = (values - center) * lax.rsqrt(spread + epsilon)
    return (normed * (1.0 + scale.astype(jnp.float32)) + shift.astype(jnp.float32)).astype(
        jnp.bfloat16
    )


def rms_gain(vectors, gain):
    factor = lax.rsqrt(jnp.mean(jnp.square(vectors), axis=-1, keepdims=True) + epsilon)
    return (vectors * factor * gain).astype(jnp.bfloat16)


LANES = 128
QUERY_BLOCK = 512
KEY_BLOCK = 1024


def attend_kernel(lengths_ref, query_ref, key_ref, value_ref, text_query_ref, text_key_ref, text_value_ref, out_ref, text_out_ref, aug_ref, text_aug_ref, *, text_len, groups, width):
    step = pl.program_id(0)
    rows = query_ref.shape[0]
    seq_len = key_ref.shape[0]

    @pl.when(step == 0)
    def _():
        for group in range(groups):
            text_lane = lax.broadcasted_iota(jnp.int32, text_value_ref.shape, 1) // width == group
            text_live = lax.broadcasted_iota(jnp.int32, text_value_ref.shape, 0) < text_len
            text_value = text_value_ref[...].astype(jnp.float32)
            text_aug_ref[group] = jnp.where(
                text_live, jnp.where(text_lane, text_value, 1.0), 0.0
            ).astype(jnp.bfloat16)

            def fill(index, carry):
                start = pl.multiple_of(index * KEY_BLOCK, KEY_BLOCK)
                shape = (KEY_BLOCK, LANES)
                own = lax.broadcasted_iota(jnp.int32, shape, 1) // width == group
                live = lax.broadcasted_iota(jnp.int32, shape, 0) + start < lengths_ref[group]
                value = value_ref[pl.ds(start, KEY_BLOCK), :].astype(jnp.float32)
                aug_ref[group, pl.ds(start, KEY_BLOCK), :] = jnp.where(
                    live, jnp.where(own, value, 1.0), 0.0
                ).astype(jnp.bfloat16)
                return carry

            lax.fori_loop(0, seq_len // KEY_BLOCK, fill, 0)

    def attend(query_from, group):
        lane = lax.broadcasted_iota(jnp.int32, query_from.shape, 1) // width
        query = jnp.where(lane == group, query_from[...].astype(jnp.float32), 0.0).astype(
            jnp.bfloat16
        )

        def part(keys, augmented):
            scores = lax.dot_general(
                query, keys, (((1,), (1,)), ((), ())), preferred_element_type=jnp.float32
            )
            weights = jnp.exp2(scores).astype(jnp.bfloat16)
            return jnp.dot(weights, augmented, preferred_element_type=jnp.float32)

        def body(index, acc):
            start = pl.multiple_of(index * KEY_BLOCK, KEY_BLOCK)
            return acc + part(
                key_ref[pl.ds(start, KEY_BLOCK), :], aug_ref[group, pl.ds(start, KEY_BLOCK), :]
            )

        acc = part(text_key_ref[...], text_aug_ref[group])
        acc = lax.fori_loop(0, (lengths_ref[group] + KEY_BLOCK - 1) // KEY_BLOCK, body, acc)
        return acc / pltpu.roll(acc, LANES // 2, 1), lane == group

    @pl.when(step == 0)
    def _():
        joined = jnp.zeros(text_out_ref.shape, jnp.float32)
        for group in range(groups):
            result, own = attend(text_query_ref, group)
            joined = jnp.where(own, result, joined)
        text_out_ref[...] = joined.astype(jnp.bfloat16)

    out_ref[...] = jnp.zeros_like(out_ref)
    row = lax.broadcasted_iota(jnp.int32, (rows, LANES), 0) + step * rows
    for group in range(groups):
        length = lengths_ref[group]

        @pl.when(step * rows < length)
        def _():
            result, own = attend(query_ref, group)
            result = jnp.where(row < length, result, 0.0).astype(jnp.bfloat16)
            out_ref[...] = jnp.where(own, result, out_ref[...])


def attend_image(lengths, by_head, text_query, text_key, text_value, text_len, groups, width):
    seq_len = by_head.shape[0]
    text_rows = text_key.shape[0]
    return pl.pallas_call(
        functools.partial(attend_kernel, text_len=text_len, groups=groups, width=width),
        grid_spec=pltpu.PrefetchScalarGridSpec(
            num_scalar_prefetch=1,
            grid=(seq_len // QUERY_BLOCK,),
            in_specs=[
                pl.BlockSpec((QUERY_BLOCK, LANES), lambda i, n: (i, 0)),
                pl.BlockSpec((seq_len, LANES), lambda i, n: (0, 1)),
                pl.BlockSpec((seq_len, LANES), lambda i, n: (0, 2)),
                pl.BlockSpec((text_rows, LANES), lambda i, n: (0, 0)),
                pl.BlockSpec((text_rows, LANES), lambda i, n: (0, 0)),
                pl.BlockSpec((text_rows, LANES), lambda i, n: (0, 0)),
            ],
            out_specs=[
                pl.BlockSpec((QUERY_BLOCK, LANES), lambda i, n: (i, 0)),
                pl.BlockSpec((text_rows, LANES), lambda i, n: (0, 0)),
            ],
            scratch_shapes=[
                pltpu.VMEM((groups, seq_len, LANES), jnp.bfloat16),
                pltpu.VMEM((groups, text_rows, LANES), jnp.bfloat16),
            ],
        ),
        out_shape=[
            jax.ShapeDtypeStruct((seq_len, LANES), jnp.bfloat16),
            jax.ShapeDtypeStruct((text_rows, LANES), jnp.bfloat16),
        ],
    )(lengths, by_head, by_head, by_head, text_query, text_key, text_value)


def local(
    image,
    text,
    pooled,
    timesteps,
    lengths,
    w_time,
    w_mod,
    w_img,
    w_txt,
    q_gain,
    k_gain,
    text_q_gain,
    text_k_gain,
):
    tile_count = lax.axis_size("tile")
    group_count, local_rows, model_width = image.shape
    seq_len = local_rows * tile_count
    text_len = text.shape[1]
    head_dim = q_gain.shape[0]
    heads_here = w_txt.shape[1] // (3 * head_dim)
    score_scale = head_dim ** (-0.5)
    same_core = [[t for t in range(tile_count) if t % 2 == c] for c in range(2)]
    all_same_core = [
        [r * tile_count + t for r in range(lax.axis_size("req")) for t in same_core[c]]
        for c in range(2)
    ]
    turned = lax.ppermute(
        w_img,
        "tile",
        [(t, t // 8 * 8 + ((t % 8) * 2 + (t % 8) // 4) % 8) for t in range(tile_count)],
    )
    w_half = lax.all_gather(
        turned, ("req", "tile"), axis=1, tiled=True, axis_index_groups=all_same_core
    )
    features = time_features(timesteps, w_time.shape[0])
    cond_act = jax.nn.silu(
        pooled + jnp.dot(features, w_time, preferred_element_type=jnp.float32)
    ).astype(jnp.bfloat16)
    mod_part = jnp.dot(cond_act, w_mod, preferred_element_type=jnp.float32).astype(jnp.bfloat16)
    modulation = lax.all_gather(mod_part, "tile", axis=1, tiled=True)
    h_img = modulate(
        image,
        modulation[:, None, 0:model_width],
        modulation[:, None, model_width : 2 * model_width],
    )
    core = lax.axis_index("tile") % 2
    h_other = lax.ppermute(h_img, "tile", [(t, t ^ 1) for t in range(tile_count)])
    h_pair = jnp.where(
        core == 0,
        jnp.concatenate([h_img, h_other], axis=1),
        jnp.concatenate([h_other, h_img], axis=1),
    )
    qkv_img = jnp.einsum("gpd,dc->gpc", h_pair, w_half, preferred_element_type=jnp.float32)
    pair_rows = 2 * local_rows
    half_heads = tile_count // 2
    qkv_img = qkv_img.reshape(group_count, pair_rows, half_heads, 3, head_dim)
    log2_scale = score_scale * math.log2(math.e)
    packed = jnp.stack(
        [
            rms_gain(qkv_img[:, :, :, 0, :], q_gain * log2_scale),
            rms_gain(qkv_img[:, :, :, 1, :], k_gain),
            qkv_img[:, :, :, 2, :].astype(jnp.bfloat16),
        ]
    )
    packed = jnp.transpose(packed, (3, 2, 0, 1, 4)).reshape(
        half_heads, pair_rows, 3 * group_count * head_dim
    )
    by_head = lax.all_to_all(
        packed, "tile", split_axis=0, concat_axis=0, tiled=True, axis_index_groups=same_core
    ).reshape(seq_len, 3 * group_count * head_dim)
    h_txt = modulate(
        text,
        modulation[:, None, 2 * model_width : 3 * model_width],
        modulation[:, None, 3 * model_width : 4 * model_width],
    )
    qkv_txt = jnp.einsum("gtd,dc->gtc", h_txt, w_txt, preferred_element_type=jnp.float32).reshape(
        group_count, text_len, heads_here, 3, head_dim
    )
    text_queries = jnp.moveaxis(rms_gain(qkv_txt[:, :, :, 0, :], text_q_gain * log2_scale), 2, 1)
    text_keys = jnp.moveaxis(rms_gain(qkv_txt[:, :, :, 1, :], text_k_gain), 2, 1)
    text_values = jnp.moveaxis(qkv_txt[:, :, :, 2, :].astype(jnp.bfloat16), 2, 1)
    text_rows = -(-text_len // 128) * 128

    def pack_text(vectors):
        joined = jnp.moveaxis(vectors[:, 0], 0, 1).reshape(text_len, group_count * head_dim)
        return jnp.pad(joined, ((0, text_rows - text_len), (0, 0)))

    image_result, text_result = attend_image(
        lengths,
        by_head,
        pack_text(text_queries),
        pack_text(text_keys),
        pack_text(text_values),
        text_len,
        group_count,
        head_dim,
    )
    sent = image_result.reshape(tile_count, local_rows, group_count * head_dim)
    got = lax.all_to_all(sent, "tile", split_axis=0, concat_axis=0, tiled=True)
    image_attention = (
        got.reshape(tile_count, local_rows, group_count, head_dim)
        .transpose(2, 1, 0, 3)
        .reshape(group_count, local_rows, tile_count * head_dim)
    )
    text_attention = jnp.moveaxis(
        text_result[:text_len].reshape(text_len, group_count, head_dim), 1, 0
    )
    return (image_attention, text_attention)


def solution(mesh):
    in_specs = (
        P("req", "tile", None),
        P("req", None, None),
        P("req", None),
        P("req"),
        P("req"),
        P(),
        P(None, "tile"),
        P(None, ("req", "tile")),
        P(None, "tile"),
        P(),
        P(),
        P(),
        P(),
    )
    out_specs = (P("req", "tile", None), P("req", None, "tile"))
    return jax.shard_map(local, mesh=mesh, in_specs=in_specs, out_specs=out_specs, check_vma=False)
```

```python
import functools
import math

import jax
import jax.numpy as jnp
from jax import lax
from jax.experimental import pallas as pl
from jax.experimental.pallas import tpu as pltpu
from jax.sharding import PartitionSpec as P

epsilon = 1e-06


def time_features(step_index, feature_count):
    half_count = feature_count // 2
    frequency = jnp.exp(-math.log(10000.0) * jnp.arange(half_count, dtype=jnp.float32) / half_count)
    angles = step_index.astype(jnp.float32)[:, None] * frequency[None, :]
    return jnp.concatenate([jnp.cos(angles), jnp.sin(angles)], axis=-1).astype(jnp.bfloat16)


def modulate(tokens, shift, scale):
    values = tokens.astype(jnp.float32)
    center = jnp.mean(values, axis=-1, keepdims=True)
    spread = jnp.mean(jnp.square(values - center), axis=-1, keepdims=True)
    normed = (values - center) * lax.rsqrt(spread + epsilon)
    return (normed * (1.0 + scale.astype(jnp.float32)) + shift.astype(jnp.float32)).astype(
        jnp.bfloat16
    )


def rms_gain(vectors, gain):
    factor = lax.rsqrt(jnp.mean(jnp.square(vectors), axis=-1, keepdims=True) + epsilon)
    return (vectors * factor * gain).astype(jnp.bfloat16)


LANES = 128
QUERY_BLOCK = 512
KEY_BLOCK = 1024


def attend_kernel(lengths_ref, query_ref, key_ref, value_ref, text_query_ref, text_key_ref, text_value_ref, out_ref, text_out_ref, aug_ref, text_aug_ref, *, text_len, groups, width):
    step = pl.program_id(0)
    rows = query_ref.shape[0]
    seq_len = key_ref.shape[0]

    @pl.when(step == 0)
    def _():
        for group in range(groups):
            text_lane = lax.broadcasted_iota(jnp.int32, text_value_ref.shape, 1) // width == group
            text_live = lax.broadcasted_iota(jnp.int32, text_value_ref.shape, 0) < text_len
            text_value = text_value_ref[...].astype(jnp.float32)
            text_aug_ref[group] = jnp.where(
                text_live, jnp.where(text_lane, text_value, 1.0), 0.0
            ).astype(jnp.bfloat16)

            def fill(index, carry):
                start = pl.multiple_of(index * KEY_BLOCK, KEY_BLOCK)
                shape = (KEY_BLOCK, LANES)
                own = lax.broadcasted_iota(jnp.int32, shape, 1) // width == group
                live = lax.broadcasted_iota(jnp.int32, shape, 0) + start < lengths_ref[group]
                value = value_ref[pl.ds(start, KEY_BLOCK), :].astype(jnp.float32)
                aug_ref[group, pl.ds(start, KEY_BLOCK), :] = jnp.where(
                    live, jnp.where(own, value, 1.0), 0.0
                ).astype(jnp.bfloat16)
                return carry

            lax.fori_loop(0, seq_len // KEY_BLOCK, fill, 0)

    def attend(query_from, group):
        lane = lax.broadcasted_iota(jnp.int32, query_from.shape, 1) // width
        query = jnp.where(lane == group, query_from[...].astype(jnp.float32), 0.0).astype(
            jnp.bfloat16
        )

        def part(keys, augmented):
            scores = lax.dot_general(
                query, keys, (((1,), (1,)), ((), ())), preferred_element_type=jnp.float32
            )
            weights = jnp.exp2(scores).astype(jnp.bfloat16)
            return jnp.dot(weights, augmented, preferred_element_type=jnp.float32)

        def body(index, acc):
            start = pl.multiple_of(index * KEY_BLOCK, KEY_BLOCK)
            return acc + part(
                key_ref[pl.ds(start, KEY_BLOCK), :], aug_ref[group, pl.ds(start, KEY_BLOCK), :]
            )

        acc = part(text_key_ref[...], text_aug_ref[group])
        acc = lax.fori_loop(0, (lengths_ref[group] + KEY_BLOCK - 1) // KEY_BLOCK, body, acc)
        return acc / pltpu.roll(acc, LANES // 2, 1), lane == group

    @pl.when(step == 0)
    def _():
        joined = jnp.zeros(text_out_ref.shape, jnp.float32)
        for group in range(groups):
            result, own = attend(text_query_ref, group)
            joined = jnp.where(own, result, joined)
        text_out_ref[...] = joined.astype(jnp.bfloat16)

    out_ref[...] = jnp.zeros_like(out_ref)
    row = lax.broadcasted_iota(jnp.int32, (rows, LANES), 0) + step * rows
    for group in range(groups):
        length = lengths_ref[group]

        @pl.when(step * rows < length)
        def _():
            result, own = attend(query_ref, group)
            result = jnp.where(row < length, result, 0.0).astype(jnp.bfloat16)
            out_ref[...] = jnp.where(own, result, out_ref[...])


def attend_image(lengths, by_head, text_query, text_key, text_value, text_len, groups, width):
    seq_len = by_head.shape[0]
    text_rows = text_key.shape[0]
    return pl.pallas_call(
        functools.partial(attend_kernel, text_len=text_len, groups=groups, width=width),
        grid_spec=pltpu.PrefetchScalarGridSpec(
            num_scalar_prefetch=1,
            grid=(seq_len // QUERY_BLOCK,),
            in_specs=[
                pl.BlockSpec((QUERY_BLOCK, LANES), lambda i, n: (i, 0)),
                pl.BlockSpec((seq_len, LANES), lambda i, n: (0, 1)),
                pl.BlockSpec((seq_len, LANES), lambda i, n: (0, 2)),
                pl.BlockSpec((text_rows, LANES), lambda i, n: (0, 0)),
                pl.BlockSpec((text_rows, LANES), lambda i, n: (0, 0)),
                pl.BlockSpec((text_rows, LANES), lambda i, n: (0, 0)),
            ],
            out_specs=[
                pl.BlockSpec((QUERY_BLOCK, LANES), lambda i, n: (i, 0)),
                pl.BlockSpec((text_rows, LANES), lambda i, n: (0, 0)),
            ],
            scratch_shapes=[
                pltpu.VMEM((groups, seq_len, LANES), jnp.bfloat16),
                pltpu.VMEM((groups, text_rows, LANES), jnp.bfloat16),
            ],
        ),
        out_shape=[
            jax.ShapeDtypeStruct((seq_len, LANES), jnp.bfloat16),
            jax.ShapeDtypeStruct((text_rows, LANES), jnp.bfloat16),
        ],
    )(lengths, by_head, by_head, by_head, text_query, text_key, text_value)


def local(
    image,
    text,
    pooled,
    timesteps,
    lengths,
    w_time,
    w_mod,
    w_img,
    w_txt,
    q_gain,
    k_gain,
    text_q_gain,
    text_k_gain,
):
    tile_count = lax.axis_size("tile")
    group_count, local_rows, model_width = image.shape
    seq_len = local_rows * tile_count
    text_len = text.shape[1]
    head_dim = q_gain.shape[0]
    heads_here = w_txt.shape[1] // (3 * head_dim)
    score_scale = head_dim ** (-0.5)
    req_count = lax.axis_size("req")
    plane = tile_count // req_count
    lines = [[x * plane + p for x in range(req_count)] for p in range(plane)]
    planes = [[x * plane + p for p in range(plane)] for x in range(req_count)]
    all_planes = [
        [r * tile_count + t for r in range(req_count) for t in planes[x]] for x in range(req_count)
    ]
    image = lax.all_gather(image, "tile", axis=1, tiled=True, axis_index_groups=lines)
    turned = lax.ppermute(
        w_img,
        ("req", "tile"),
        [
            (r * tile_count + x * plane + p, x * tile_count + r * plane + p)
            for r in range(req_count)
            for x in range(req_count)
            for p in range(plane)
        ],
    )
    w_part = lax.all_gather(
        turned, ("req", "tile"), axis=1, tiled=True, axis_index_groups=all_planes
    )
    features = time_features(timesteps, w_time.shape[0])
    cond_act = jax.nn.silu(
        pooled + jnp.dot(features, w_time, preferred_element_type=jnp.float32)
    ).astype(jnp.bfloat16)
    mod_part = jnp.dot(cond_act, w_mod, preferred_element_type=jnp.float32).astype(jnp.bfloat16)
    modulation = lax.all_gather(mod_part, "tile", axis=1, tiled=True)
    h_img = modulate(
        image,
        modulation[:, None, 0:model_width],
        modulation[:, None, model_width : 2 * model_width],
    )
    qkv_img = jnp.einsum("gpd,dc->gpc", h_img, w_part, preferred_element_type=jnp.float32)
    line_rows = req_count * local_rows
    qkv_img = qkv_img.reshape(group_count, line_rows, plane, 3, head_dim)
    log2_scale = score_scale * math.log2(math.e)
    packed = jnp.stack(
        [
            rms_gain(qkv_img[:, :, :, 0, :], q_gain * log2_scale),
            rms_gain(qkv_img[:, :, :, 1, :], k_gain),
            qkv_img[:, :, :, 2, :].astype(jnp.bfloat16),
        ]
    )
    packed = jnp.transpose(packed, (3, 2, 0, 1, 4)).reshape(
        plane, line_rows, 3 * group_count * head_dim
    )
    by_head = lax.all_to_all(
        packed, "tile", split_axis=0, concat_axis=0, tiled=True, axis_index_groups=planes
    )
    by_head = (
        by_head.reshape(plane, req_count, local_rows, 3 * group_count * head_dim)
        .swapaxes(0, 1)
        .reshape(seq_len, 3 * group_count * head_dim)
    )
    h_txt = modulate(
        text,
        modulation[:, None, 2 * model_width : 3 * model_width],
        modulation[:, None, 3 * model_width : 4 * model_width],
    )
    qkv_txt = jnp.einsum("gtd,dc->gtc", h_txt, w_txt, preferred_element_type=jnp.float32).reshape(
        group_count, text_len, heads_here, 3, head_dim
    )
    text_queries = jnp.moveaxis(rms_gain(qkv_txt[:, :, :, 0, :], text_q_gain * log2_scale), 2, 1)
    text_keys = jnp.moveaxis(rms_gain(qkv_txt[:, :, :, 1, :], text_k_gain), 2, 1)
    text_values = jnp.moveaxis(qkv_txt[:, :, :, 2, :].astype(jnp.bfloat16), 2, 1)
    text_rows = -(-text_len // 128) * 128

    def pack_text(vectors):
        joined = jnp.moveaxis(vectors[:, 0], 0, 1).reshape(text_len, group_count * head_dim)
        return jnp.pad(joined, ((0, text_rows - text_len), (0, 0)))

    image_result, text_result = attend_image(
        lengths,
        by_head,
        pack_text(text_queries),
        pack_text(text_keys),
        pack_text(text_values),
        text_len,
        group_count,
        head_dim,
    )
    sent = image_result.reshape(tile_count, local_rows, group_count * head_dim)
    got = lax.all_to_all(sent, "tile", split_axis=0, concat_axis=0, tiled=True)
    image_attention = (
        got.reshape(tile_count, local_rows, group_count, head_dim)
        .transpose(2, 1, 0, 3)
        .reshape(group_count, local_rows, tile_count * head_dim)
    )
    text_attention = jnp.moveaxis(
        text_result[:text_len].reshape(text_len, group_count, head_dim), 1, 0
    )
    return (image_attention, text_attention)


def solution(mesh):
    in_specs = (
        P("req", "tile", None),
        P("req", None, None),
        P("req", None),
        P("req"),
        P("req"),
        P(),
        P(None, "tile"),
        P(None, ("req", "tile")),
        P(None, "tile"),
        P(),
        P(),
        P(),
        P(),
    )
    out_specs = (P("req", "tile", None), P("req", None, "tile"))
    return jax.shard_map(local, mesh=mesh, in_specs=in_specs, out_specs=out_specs, check_vma=False)
```

```python
import functools
import math

import jax
import jax.numpy as jnp
from jax import lax
from jax.experimental import pallas as pl
from jax.experimental.pallas import tpu as pltpu
from jax.sharding import PartitionSpec as P

epsilon = 1e-06


def time_features(step_index, feature_count):
    half_count = feature_count // 2
    frequency = jnp.exp(-math.log(10000.0) * jnp.arange(half_count, dtype=jnp.float32) / half_count)
    angles = step_index.astype(jnp.float32)[:, None] * frequency[None, :]
    return jnp.concatenate([jnp.cos(angles), jnp.sin(angles)], axis=-1).astype(jnp.bfloat16)


def modulate(tokens, shift, scale):
    values = tokens.astype(jnp.float32)
    center = jnp.mean(values, axis=-1, keepdims=True)
    spread = jnp.mean(jnp.square(values - center), axis=-1, keepdims=True)
    normed = (values - center) * lax.rsqrt(spread + epsilon)
    return (normed * (1.0 + scale.astype(jnp.float32)) + shift.astype(jnp.float32)).astype(
        jnp.bfloat16
    )


def rms_gain(vectors, gain):
    factor = lax.rsqrt(jnp.mean(jnp.square(vectors), axis=-1, keepdims=True) + epsilon)
    return (vectors * factor * gain).astype(jnp.bfloat16)


LANES = 128
QUERY_BLOCK = 512
KEY_BLOCK = 1024


def attend_kernel(lengths_ref, query_ref, key_ref, value_ref, text_query_ref, text_key_ref, text_value_ref, out_ref, text_out_ref, aug_ref, text_aug_ref, *, text_len, groups, width):
    step = pl.program_id(0)
    rows = query_ref.shape[0]
    seq_len = key_ref.shape[0]

    @pl.when(step == 0)
    def _():
        for group in range(groups):
            text_lane = lax.broadcasted_iota(jnp.int32, text_value_ref.shape, 1) // width == group
            text_live = lax.broadcasted_iota(jnp.int32, text_value_ref.shape, 0) < text_len
            text_value = text_value_ref[...].astype(jnp.float32)
            text_aug_ref[group] = jnp.where(
                text_live, jnp.where(text_lane, text_value, 1.0), 0.0
            ).astype(jnp.bfloat16)

            def fill(index, carry):
                start = pl.multiple_of(index * KEY_BLOCK, KEY_BLOCK)
                shape = (KEY_BLOCK, LANES)
                own = lax.broadcasted_iota(jnp.int32, shape, 1) // width == group
                live = lax.broadcasted_iota(jnp.int32, shape, 0) + start < lengths_ref[group]
                value = value_ref[pl.ds(start, KEY_BLOCK), :].astype(jnp.float32)
                aug_ref[group, pl.ds(start, KEY_BLOCK), :] = jnp.where(
                    live, jnp.where(own, value, 1.0), 0.0
                ).astype(jnp.bfloat16)
                return carry

            lax.fori_loop(0, seq_len // KEY_BLOCK, fill, 0)

    def attend(query_from, group):
        lane = lax.broadcasted_iota(jnp.int32, query_from.shape, 1) // width
        query = jnp.where(lane == group, query_from[...].astype(jnp.float32), 0.0).astype(
            jnp.bfloat16
        )

        def part(keys, augmented):
            scores = lax.dot_general(
                query, keys, (((1,), (1,)), ((), ())), preferred_element_type=jnp.float32
            )
            weights = jnp.exp2(scores).astype(jnp.bfloat16)
            return jnp.dot(weights, augmented, preferred_element_type=jnp.float32)

        def body(index, acc):
            start = pl.multiple_of(index * KEY_BLOCK, KEY_BLOCK)
            return acc + part(
                key_ref[pl.ds(start, KEY_BLOCK), :], aug_ref[group, pl.ds(start, KEY_BLOCK), :]
            )

        acc = part(text_key_ref[...], text_aug_ref[group])
        acc = lax.fori_loop(0, (lengths_ref[group] + KEY_BLOCK - 1) // KEY_BLOCK, body, acc)
        return acc / pltpu.roll(acc, LANES // 2, 1), lane == group

    @pl.when(step == 0)
    def _():
        joined = jnp.zeros(text_out_ref.shape, jnp.float32)
        for group in range(groups):
            result, own = attend(text_query_ref, group)
            joined = jnp.where(own, result, joined)
        text_out_ref[...] = joined.astype(jnp.bfloat16)

    out_ref[...] = jnp.zeros_like(out_ref)
    row = lax.broadcasted_iota(jnp.int32, (rows, LANES), 0) + step * rows
    for group in range(groups):
        length = lengths_ref[group]

        @pl.when(step * rows < length)
        def _():
            result, own = attend(query_ref, group)
            result = jnp.where(row < length, result, 0.0).astype(jnp.bfloat16)
            out_ref[...] = jnp.where(own, result, out_ref[...])


def attend_image(lengths, by_head, text_query, text_key, text_value, text_len, groups, width):
    seq_len = by_head.shape[0]
    text_rows = text_key.shape[0]
    return pl.pallas_call(
        functools.partial(attend_kernel, text_len=text_len, groups=groups, width=width),
        grid_spec=pltpu.PrefetchScalarGridSpec(
            num_scalar_prefetch=1,
            grid=(seq_len // QUERY_BLOCK,),
            in_specs=[
                pl.BlockSpec((QUERY_BLOCK, LANES), lambda i, n: (i, 0)),
                pl.BlockSpec((seq_len, LANES), lambda i, n: (0, 1)),
                pl.BlockSpec((seq_len, LANES), lambda i, n: (0, 2)),
                pl.BlockSpec((text_rows, LANES), lambda i, n: (0, 0)),
                pl.BlockSpec((text_rows, LANES), lambda i, n: (0, 0)),
                pl.BlockSpec((text_rows, LANES), lambda i, n: (0, 0)),
            ],
            out_specs=[
                pl.BlockSpec((QUERY_BLOCK, LANES), lambda i, n: (i, 0)),
                pl.BlockSpec((text_rows, LANES), lambda i, n: (0, 0)),
            ],
            scratch_shapes=[
                pltpu.VMEM((groups, seq_len, LANES), jnp.bfloat16),
                pltpu.VMEM((groups, text_rows, LANES), jnp.bfloat16),
            ],
        ),
        out_shape=[
            jax.ShapeDtypeStruct((seq_len, LANES), jnp.bfloat16),
            jax.ShapeDtypeStruct((text_rows, LANES), jnp.bfloat16),
        ],
    )(lengths, by_head, by_head, by_head, text_query, text_key, text_value)


def local(
    image,
    text,
    pooled,
    timesteps,
    lengths,
    w_time,
    w_mod,
    w_img,
    w_txt,
    q_gain,
    k_gain,
    text_q_gain,
    text_k_gain,
):
    tile_count = lax.axis_size("tile")
    group_count, local_rows, model_width = image.shape
    seq_len = local_rows * tile_count
    text_len = text.shape[1]
    head_dim = q_gain.shape[0]
    heads_here = w_txt.shape[1] // (3 * head_dim)
    score_scale = head_dim ** (-0.5)
    req_count = lax.axis_size("req")
    plane = tile_count // req_count
    planes = [[x * plane + p for p in range(plane)] for x in range(req_count)]
    all_planes = [
        [r * tile_count + t for r in range(req_count) for t in planes[x]] for x in range(req_count)
    ]
    ahead = [(t, (t + plane) % tile_count) for t in range(tile_count)]
    back = [(to, at) for at, to in ahead]
    from_last = lax.ppermute(image, "tile", ahead)
    from_next = lax.ppermute(image, "tile", back)
    half_group = group_count // 2
    far_low = lax.ppermute(from_next[:half_group], "tile", back)
    far_high = lax.ppermute(from_last[half_group:], "tile", ahead)
    image = jnp.concatenate(
        [image, from_next, jnp.concatenate([far_low, far_high], axis=0), from_last], axis=1
    )
    turned = lax.ppermute(
        w_img,
        ("req", "tile"),
        [
            (r * tile_count + x * plane + p, x * tile_count + r * plane + p)
            for r in range(req_count)
            for x in range(req_count)
            for p in range(plane)
        ],
    )
    w_part = lax.all_gather(
        turned, ("req", "tile"), axis=1, tiled=True, axis_index_groups=all_planes
    )
    features = time_features(timesteps, w_time.shape[0])
    cond_act = jax.nn.silu(
        pooled + jnp.dot(features, w_time, preferred_element_type=jnp.float32)
    ).astype(jnp.bfloat16)
    mod_part = jnp.dot(cond_act, w_mod, preferred_element_type=jnp.float32).astype(jnp.bfloat16)
    modulation = lax.all_gather(mod_part, "tile", axis=1, tiled=True)
    h_img = modulate(
        image,
        modulation[:, None, 0:model_width],
        modulation[:, None, model_width : 2 * model_width],
    )
    qkv_img = jnp.einsum("gpd,dc->gpc", h_img, w_part, preferred_element_type=jnp.float32)
    line_rows = req_count * local_rows
    qkv_img = qkv_img.reshape(group_count, line_rows, plane, 3, head_dim)
    log2_scale = score_scale * math.log2(math.e)
    packed = jnp.stack(
        [
            rms_gain(qkv_img[:, :, :, 0, :], q_gain * log2_scale),
            rms_gain(qkv_img[:, :, :, 1, :], k_gain),
            qkv_img[:, :, :, 2, :].astype(jnp.bfloat16),
        ]
    )
    packed = jnp.transpose(packed, (3, 2, 0, 1, 4)).reshape(
        plane, line_rows, 3 * group_count * head_dim
    )
    by_head = lax.all_to_all(
        packed, "tile", split_axis=0, concat_axis=0, tiled=True, axis_index_groups=planes
    )
    by_head = (
        jnp.roll(
            by_head.reshape(plane, req_count, local_rows, 3 * group_count * head_dim).swapaxes(0, 1),
            lax.axis_index("tile") // plane,
            axis=0,
        )
    ).reshape(seq_len, 3 * group_count * head_dim)
    h_txt = modulate(
        text,
        modulation[:, None, 2 * model_width : 3 * model_width],
        modulation[:, None, 3 * model_width : 4 * model_width],
    )
    qkv_txt = jnp.einsum("gtd,dc->gtc", h_txt, w_txt, preferred_element_type=jnp.float32).reshape(
        group_count, text_len, heads_here, 3, head_dim
    )
    text_queries = jnp.moveaxis(rms_gain(qkv_txt[:, :, :, 0, :], text_q_gain * log2_scale), 2, 1)
    text_keys = jnp.moveaxis(rms_gain(qkv_txt[:, :, :, 1, :], text_k_gain), 2, 1)
    text_values = jnp.moveaxis(qkv_txt[:, :, :, 2, :].astype(jnp.bfloat16), 2, 1)
    text_rows = -(-text_len // 128) * 128

    def pack_text(vectors):
        joined = jnp.moveaxis(vectors[:, 0], 0, 1).reshape(text_len, group_count * head_dim)
        return jnp.pad(joined, ((0, text_rows - text_len), (0, 0)))

    image_result, text_result = attend_image(
        lengths,
        by_head,
        pack_text(text_queries),
        pack_text(text_keys),
        pack_text(text_values),
        text_len,
        group_count,
        head_dim,
    )
    sent = image_result.reshape(tile_count, local_rows, group_count * head_dim)
    got = lax.all_to_all(sent, "tile", split_axis=0, concat_axis=0, tiled=True)
    image_attention = (
        got.reshape(tile_count, local_rows, group_count, head_dim)
        .transpose(2, 1, 0, 3)
        .reshape(group_count, local_rows, tile_count * head_dim)
    )
    text_attention = jnp.moveaxis(
        text_result[:text_len].reshape(text_len, group_count, head_dim), 1, 0
    )
    return (image_attention, text_attention)


def solution(mesh):
    in_specs = (
        P("req", "tile", None),
        P("req", None, None),
        P("req", None),
        P("req"),
        P("req"),
        P(),
        P(None, "tile"),
        P(None, ("req", "tile")),
        P(None, "tile"),
        P(),
        P(),
        P(),
        P(),
    )
    out_specs = (P("req", "tile", None), P("req", None, "tile"))
    return jax.shard_map(local, mesh=mesh, in_specs=in_specs, out_specs=out_specs, check_vma=False)
```
